128 devices in a mesh: dp: 32 (over x, y, core), pair: 4 (over z).
Axes of the slice: x: 4, y: 4, z: 4, core: 2. Of those that a mesh axis runs over, the one named last changes fastest.
Arguments:
- local_grads: bfloat16 [128, 1536, 4096], P(('dp', 'pair')), may hold values from -512 to 512, as said below
- error_feedback: bfloat16 [128, 1536, 4096], P(('dp', 'pair')), may hold values from -6 to 6
- q_start: float32 [4096, 32], replicated, may hold values from -0.09375 to 0.09375
Outputs:
- left_out: float32 [1536, 32], P(('dp', 'pair'))
- right_out: float32 [4096, 32], P(('dp', 'pair'))
The draws below stay inside these ranges and needn't reach their ends.
Inputs may be any that keep to these rules, and one draw needn't show every extreme that they name: `local_grads`: each replica's own gradient.
All inputs are finite; a program needn't handle non-finite values.
Results may differ from the reference program's by a relative error of at most 0.0003.
Values sent between devices are 32-bit elements; how exact they have to be, the bound alone decides.
A program may use at most 128 MiB of HBM per device.

```python
import math
import jax
import jax.numpy as jnp
from jax import lax

D = 1536
FF = 4096
RANK = 32
ITERS = 2
NREP = 128


def draw_local_grads(key, part):
    key_rows, key_cols, key_noise = jax.random.split(key, 3)
    trend = jnp.exp(math.log(3.0) * jnp.arange(D, dtype=jnp.float32) / (D - 1))
    row_scale = trend * jnp.exp(math.log(4.0) * jax.random.uniform(key_rows, (D,), jnp.float32))
    col_scale = jnp.exp(math.log(10.0) * jax.random.uniform(key_cols, (FF,), jnp.float32))
    noise = jax.random.truncated_normal(key_noise, -6.0, 6.0, (NREP, D, FF), jnp.float32)
    values = noise * 0.5
    return (values * row_scale[None, :, None] * col_scale[None, None, :]).astype(jnp.bfloat16)


def steps_of(own_key, extent, shards, least, largest):
    def one(position, parts):
        draws = jax.random.uniform(jax.random.fold_in(jax.random.fold_in(own_key, 6), position), (parts,), jnp.float32, least / len(shards), largest / len(shards))
        return jnp.repeat(jnp.exp(draws), extent[position] // parts).reshape((-1,) + (1,) * (len(extent) - position - 1))

    level = one(*shards[0])
    for cut in shards[1:]:
        level = level * one(*cut)
    return level


def normal_values(stream_key, dims, deviation, limit, shards=(), held_as=jnp.bfloat16):
    factor_of = steps_of(stream_key, dims, shards, -0.22, 0.18) if shards else 1.0
    entries = jax.random.normal(stream_key, dims, jnp.float32) * deviation * factor_of
    return jnp.minimum(jnp.maximum(entries, -limit), limit).astype(held_as)


def setup_inputs(seed: int = 0) -> dict:
    key_of = jax.random.split(jax.random.key(seed), 4)
    local_grads = draw_local_grads(jax.random.fold_in(key_of[3], 71), 0)
    error_feedback = normal_values(key_of[1], (NREP, D, FF), 1.0, 6.0, ((0, 128),))
    q_start = normal_values(key_of[2], (FF, RANK), FF ** -0.5, 0.09375, (), jnp.float32)
    return {"local_grads": local_grads, "error_feedback": error_feedback, "q_start": q_start}


def orthonormal(factor):
    gram_matrix = jnp.dot(factor.T, factor, precision=lax.Precision.HIGHEST)
    lower_factor = jnp.linalg.cholesky(gram_matrix)
    return jax.scipy.linalg.solve_triangular(lower_factor, factor.T, lower=True).T

def left_sum(local_grads, error_feedback, basis_now):

    def accumulate(carry_sum, slices):
        merged = slices[0].astype(jnp.float32) + slices[1].astype(jnp.float32)
        return (carry_sum + jnp.dot(merged, basis_now, precision=lax.Precision.HIGHEST), None)
    result, unused = lax.scan(accumulate, jnp.zeros((D, RANK), jnp.float32), (local_grads, error_feedback))
    return result

def right_sum(local_grads, error_feedback, left_basis):

    def accumulate(carry_sum, slices):
        merged = slices[0].astype(jnp.float32) + slices[1].astype(jnp.float32)
        term = lax.dot_general(merged, left_basis, (((0,), (0,)), ((), ())), precision=lax.Precision.HIGHEST)
        return (carry_sum + term, None)
    result, unused = lax.scan(accumulate, jnp.zeros((FF, RANK), jnp.float32), (local_grads, error_feedback))
    return result

def reference(local_grads, error_feedback, q_start):
    replicas = local_grads.shape[0]
    basis_now = q_start
    left_factor = None
    right_factor = None
    for iteration in range(ITERS):
        left_factor = left_sum(local_grads, error_feedback, basis_now) / replicas
        left_basis = orthonormal(left_factor)
        right_factor = right_sum(local_grads, error_feedback, left_basis) / replicas
        if iteration + 1 < ITERS:
            basis_now = orthonormal(right_factor)
    return (left_factor, right_factor)
```

```python
import jax
import jax.numpy as jnp
from jax import lax
from jax.experimental import pallas as pl
from jax.experimental.pallas import tpu as pltpu
from jax.sharding import PartitionSpec as P

MESH = pl.DeviceIdType.MESH
F32 = jnp.float32
BF16 = jnp.bfloat16
EXACT = lax.Precision.HIGHEST

X, Y, CORES, PAIR = 4, 4, 2, 4
N = X * Y * CORES * PAIR
D, FF, RANK = 1536, 4096, 32
PARTS = 3
GROUPS = RANK // 8
TL = D // 128 * GROUPS
ROWS = 256
COLS = 512
SCALE = 1.0 / N
OUT_L, OUT_R = D // N, FF // N

NT = (((1,), (1,)), ((), ()))


def device(i):
    return (i // PAIR, i % PAIR)


def position():
    return lax.axis_index("dp") * PAIR + lax.axis_index("pair")


def owner_of_left(t):
    return (t * N) // TL


def far_first(k):
    dp, z = lax.axis_index("dp"), lax.axis_index("pair")
    x, y, c = dp // (Y * CORES), (dp // CORES) % Y, dp % CORES

    def step(t):
        return ((3 - t) * (4 - t) // 2) % 4

    x = (x + step(k // 32)) % X
    y = (y + step((k // 8) % 4)) % Y
    z = (z + step((k // 2) % 4)) % PAIR
    c = (c + 1 - k % 2) % CORES
    return ((x * Y + y) * CORES + c, z)


def split(x):
    high = x.astype(BF16)
    rest = x - high.astype(F32)
    mid = rest.astype(BF16)
    low = (rest - mid.astype(F32)).astype(BF16)
    return high, mid, low


def put_parts(ref, columns, x):
    for i, part in enumerate(split(x)):
        ref[i * RANK:(i + 1) * RANK, columns] = part


def add_parts(acc):
    return (acc[2 * RANK:3 * RANK] + acc[RANK:2 * RANK]) + acc[0:RANK]


def lane_group(shape):
    return lax.broadcasted_iota(jnp.int32, shape, 1) // RANK


def regroup(tiles, to):
    group = lane_group((8, 128))
    out = None
    for q, tile in enumerate(tiles):
        moved = pltpu.roll(tile, (RANK * (q - to)) % 128, 1) if q != to else tile
        out = moved if out is None else jnp.where(group == q, moved, out)
    return out


def inverse_factor(parts_ref):
    gram = lax.dot_general(parts_ref[0:PARTS * RANK, :], parts_ref[...], NT, preferred_element_type=F32)
    gram = add_parts(gram)
    gram = (pltpu.roll(gram, 64, 1) + pltpu.roll(gram, 96, 1)) + gram
    lane = lax.broadcasted_iota(jnp.int32, (RANK, 128), 1)
    row = lax.broadcasted_iota(jnp.int32, (RANK, 128), 0)
    both = jnp.where(lane < RANK, gram, jnp.where(lane == row + RANK, 1.0, 0.0))
    for k in range(RANK - 1):
        pivot_row = both[k:k + 1, :]
        scaled = pivot_row / both[k:k + 1, k:k + 1]
        factor = jnp.where(row > k, jnp.broadcast_to(both[:, k:k + 1], (RANK, 128)), 0.0)
        both = both - factor * scaled
    pivots = jnp.sum(jnp.where(lane == row, both, 0.0), axis=1, keepdims=True)
    return (pltpu.roll(both, 96, 1) / jnp.sqrt(pivots))[:, 0:RANK]


def total(ref):
    sums = [jnp.sum(ref[i * 16:(i + 1) * 16], axis=0) for i in range(N // 16)]
    while len(sums) > 1:
        sums = [a + b for a, b in zip(sums[::2], sums[1::2])]
    return sums[0] * SCALE


def wait_tiles(ref, count, sem):
    pltpu.make_async_copy(ref.at[pl.ds(0, count)], ref.at[pl.ds(0, count)], sem).wait()


def kernel(
    grads, errors, start, left_out, right_out,
    g, e, q, b_parts, l_parts, l_send, l_recv, l_all, r_send, r_recv, r_all, tile, left, load_sem, send_sem, recv_sem,
):
    me = position()
    my_left = (me * TL + N - 1) // N
    owns_left = jnp.logical_and(my_left < TL, owner_of_left(my_left) == me)
    chunks = D // ROWS
    first_chunk = (me * chunks) // N + chunks // 2

    def load(i):
        rows = pl.ds(pl.multiple_of(((first_chunk + i) % chunks) * ROWS, ROWS), ROWS)
        return (
            pltpu.make_async_copy(grads.at[0, rows, :], g.at[rows, :], load_sem.at[i]),
            pltpu.make_async_copy(errors.at[0, rows, :], e.at[rows, :], load_sem.at[chunks + i]),
        )

    q_copy = pltpu.make_async_copy(start, q, load_sem.at[2 * chunks])
    q_copy.start()
    for i in range(chunks):
        for copy in load(i):
            copy.start()

    barrier = pltpu.get_barrier_semaphore()

    def greet(k, carry):
        pl.semaphore_signal(barrier, inc=1, device_id=device((me + k) % N), device_id_type=MESH)
        return carry

    lax.fori_loop(1, N, greet, 0)

    b_parts[PARTS * RANK:, :] = jnp.zeros((128 - PARTS * RANK, FF), BF16)
    l_parts[PARTS * RANK:, :] = jnp.zeros((128 - PARTS * RANK, D), BF16)
    left[:, D:] = jnp.zeros((RANK, 128), F32)
    q_copy.wait()

    def turn(j, carry):
        rows = pl.ds(pl.multiple_of(j * 128, 128), 128)
        put_parts(b_parts, rows, q[rows, :].T)
        return carry

    lax.fori_loop(0, FF // 128, turn, 0)

    def to_left_owner(it, t):
        owner = owner_of_left(t)

        @pl.when(owner != me)
        def _():
            pltpu.make_async_remote_copy(
                l_send.at[it, t], l_recv.at[it, me], send_sem.at[2 * it], recv_sem.at[2 * it],
                device_id=device(owner), device_id_type=MESH,
            ).start()

        @pl.when(owner == me)
        def _():
            l_recv[it, me] = l_send[it, t]

    def left_chunk(it, i):
        chunk = (first_chunk + i) % chunks
        rows = pl.ds(pl.multiple_of(chunk * ROWS, ROWS), ROWS)
        parts = b_parts[0:PARTS * RANK, :]
        acc = lax.dot_general(parts, g[rows, :], NT, preferred_element_type=F32)
        acc = acc + lax.dot_general(parts, e[rows, :], NT, preferred_element_type=F32)
        acc = add_parts(acc)
        tiles = ROWS // 128 * GROUPS
        for j in range(tiles):
            lanes = slice(j // GROUPS * 128, j // GROUPS * 128 + 128)
            ranks = slice(j % GROUPS * 8, j % GROUPS * 8 + 8)
            l_send[it, chunk * tiles + j] = acc[ranks, lanes]

        def send(j, carry):
            to_left_owner(it, chunk * tiles + j)
            return carry

        lax.fori_loop(0, tiles, send, 0)

    def right_chunk(it, i):
        steps = FF // COLS
        chunk = ((me * steps) // N + steps // 2 + i) % steps
        columns = pl.ds(pl.multiple_of(chunk * COLS, COLS), COLS)
        parts = l_parts[0:PARTS * RANK, :]
        acc = jnp.dot(parts, g[:, columns], preferred_element_type=F32)
        acc = acc + jnp.dot(parts, e[:, columns], preferred_element_type=F32)
        acc = add_parts(acc)
        owners = COLS // OUT_R
        for j in range(COLS // 128):
            tiles = [acc[r * 8:r * 8 + 8, j * 128:j * 128 + 128] for r in range(GROUPS)]
            for r in range(128 // OUT_R):
                r_send[it, chunk * owners + j * (128 // OUT_R) + r] = regroup(tiles, r)

        def send(j, carry):
            owner = chunk * owners + j

            @pl.when(owner != me)
            def _():
                pltpu.make_async_remote_copy(
                    r_send.at[it, owner], r_recv.at[it, me], send_sem.at[2 * it + 1], recv_sem.at[2 * it + 1],
                    device_id=device(owner), device_id_type=MESH,
                ).start()

            @pl.when(owner == me)
            def _():
                r_recv[it, me] = r_send[it, owner]

            return carry

        lax.fori_loop(0, owners, send, 0)

    def send_left_sums(it):
        @pl.when(owns_left)
        def _():
            wait_tiles(l_recv.at[it], N - 1, recv_sem.at[2 * it])
            tile[it] = total(l_recv.at[it])

            def send(k, carry):
                pltpu.make_async_remote_copy(
                    tile.at[it], l_all.at[it, my_left], send_sem.at[4 + it], recv_sem.at[4 + it],
                    device_id=far_first(k), device_id_type=MESH,
                ).start()
                return carry

            lax.fori_loop(0, N - 1, send, 0)
            l_all[it, my_left] = tile[it]
            wait_tiles(l_all.at[it], TL - 1, recv_sem.at[4 + it])

        @pl.when(jnp.logical_not(owns_left))
        def _():
            wait_tiles(l_all.at[it], TL, recv_sem.at[4 + it])

    def right_sum(it, inverse):
        wait_tiles(r_recv.at[it], N - 1, recv_sem.at[2 * it + 1])
        summed = total(r_recv.at[it])
        ranks = [pltpu.roll(summed, (128 - RANK * r) % 128, 1) if r else summed for r in range(GROUPS)]
        return jnp.dot(inverse, jnp.concatenate(ranks, axis=0), precision=EXACT, preferred_element_type=F32)

    for i in range(chunks):
        for copy in load(i):
            copy.wait()
        if i == 0:
            pl.semaphore_wait(barrier, N - 1)
        left_chunk(0, i)
    send_left_sums(0)
    for j in range(D // 128):
        block = jnp.concatenate([l_all[0, j * GROUPS + r] for r in range(GROUPS)], axis=0)
        put_parts(l_parts, slice(j * 128, j * 128 + 128), block)
    lax.fori_loop(0, FF // COLS, lambda i, carry: (right_chunk(0, i), carry)[1], 0)
    inverse = inverse_factor(l_parts)
    mine = right_sum(0, inverse)
    packed = mine[0:8]
    group = lane_group((8, 128))
    for r in range(1, GROUPS):
        packed = jnp.where(group == r, pltpu.roll(mine[r * 8:r * 8 + 8], RANK * r, 1), packed)
    tile[2] = packed

    def send_right(k, carry):
        pltpu.make_async_remote_copy(
            tile.at[2], r_all.at[me], send_sem.at[6], recv_sem.at[6],
            device_id=far_first(k), device_id_type=MESH,
        ).start()
        return carry

    lax.fori_loop(0, N - 1, send_right, 0)
    r_all[me] = tile[2]
    wait_tiles(r_all, N - 1, recv_sem.at[6])

    def gather_right(j, carry):
        tiles = [r_all[j * 4 + r] for r in range(4)]
        block = jnp.concatenate([regroup(tiles, r) for r in range(GROUPS)], axis=0)
        put_parts(b_parts, pl.ds(pl.multiple_of(j * 128, 128), 128), block)
        return carry

    lax.fori_loop(0, FF // 128, gather_right, 0)

    lax.fori_loop(0, chunks, lambda i, carry: (left_chunk(1, i), carry)[1], 0)
    inverse = inverse_factor(b_parts)
    send_left_sums(1)
    for j in range(D // 512):
        block = jnp.concatenate(
            [
                jnp.concatenate([l_all[1, (j * 4 + i) * GROUPS + r] for r in range(GROUPS)], axis=0)
                for i in range(4)
            ],
            axis=1,
        )
        block = jnp.dot(inverse, block, precision=EXACT, preferred_element_type=F32)
        left[:, j * 512:j * 512 + 512] = block
        put_parts(l_parts, slice(j * 512, j * 512 + 512), block)
    lax.fori_loop(0, FF // COLS, lambda i, carry: (right_chunk(1, i), carry)[1], 0)
    at = (me * OUT_L) // 128
    block = left[:, pl.ds(pl.multiple_of(at * 128, 128), 256)]
    block = pltpu.roll(block, (256 - (me * OUT_L - at * 128)) % 256, 1)[:, 0:128]
    left_out[...] = block.T[0:OUT_L, :]
    inverse = inverse_factor(l_parts)
    mine = right_sum(1, inverse)
    right_out[...] = mine.T[0:OUT_R, :]

    for it in range(2):
        @pl.when(owns_left)
        def _():
            wait_tiles(l_send.at[it], TL - 1, send_sem.at[2 * it])
            wait_tiles(r_send.at[it], N - 1, send_sem.at[4 + it])

        @pl.when(jnp.logical_not(owns_left))
        def _():
            wait_tiles(l_send.at[it], TL, send_sem.at[2 * it])

        wait_tiles(r_send.at[it], N - 1, send_sem.at[2 * it + 1])
    wait_tiles(r_all, N - 1, send_sem.at[6])


def shards(local_grads, error_feedback, q_start):
    anywhere = pl.BlockSpec(memory_space=pl.ANY)
    vmem = pl.BlockSpec(memory_space=pltpu.VMEM)
    return pl.pallas_call(
        kernel,
        out_shape=(
            jax.ShapeDtypeStruct((OUT_L, RANK), F32),
            jax.ShapeDtypeStruct((OUT_R, RANK), F32),
        ),
        in_specs=[anywhere, anywhere, anywhere],
        out_specs=(vmem, vmem),
        scratch_shapes=[
            pltpu.VMEM((D, FF), BF16),
            pltpu.VMEM((D, FF), BF16),
            pltpu.VMEM((FF, RANK), F32),
            pltpu.VMEM((128, FF), BF16),
            pltpu.VMEM((128, D), BF16),
            pltpu.VMEM((2, TL, 8, 128), F32),
            pltpu.VMEM((2, N, 8, 128), F32),
            pltpu.VMEM((2, TL, 8, 128), F32),
            pltpu.VMEM((2, N, 8, 128), F32),
            pltpu.VMEM((2, N, 8, 128), F32),
            pltpu.VMEM((N, 8, 128), F32),
            pltpu.VMEM((3, 8, 128), F32),
            pltpu.VMEM((RANK, D + 128), F32),
            pltpu.SemaphoreType.DMA((2 * (D // ROWS) + 1,)),
            pltpu.SemaphoreType.DMA((7,)),
            pltpu.SemaphoreType.DMA((7,)),
        ],
        compiler_params=pltpu.CompilerParams(
            vmem_limit_bytes=60 << 20, collective_id=0, has_side_effects=True
        ),
    )(local_grads, error_feedback, q_start)


def solution(mesh):
    return jax.shard_map(
        shards,
        mesh=mesh,
        in_specs=(P(("dp", "pair"), None, None), P(("dp", "pair"), None, None), P()),
        out_specs=(P(("dp", "pair"), None), P(("dp", "pair"), None)),
        check_vma=False,
    )
```

```python
import jax
import jax.numpy as jnp
from jax import lax
from jax.experimental import pallas as pl
from jax.experimental.pallas import tpu as pltpu
from jax.sharding import PartitionSpec as P

MESH = pl.DeviceIdType.MESH
F32 = jnp.float32
BF16 = jnp.bfloat16
EXACT = lax.Precision.HIGHEST

X, Y, CORES, PAIR = 4, 4, 2, 4
N = X * Y * CORES * PAIR
D, FF, RANK = 1536, 4096, 32
PARTS = 3
GROUPS = RANK // 8
TL = D // 128 * GROUPS
ROWS = 256
ROWS2 = 512
COLS = 1024
ROWS2 = 512
STEPS_X = FF // COLS
CHIPS = N // CORES
PLANE = CHIPS // X
SCALE = 1.0 / N
OUT_L, OUT_R = D // N, FF // N
OUT_AT = -(-OUT_L // 8) * 8

NT = (((1,), (1,)), ((), ()))


def device(i):
    return (i // PAIR, i % PAIR)


def position():
    return lax.axis_index("dp") * PAIR + lax.axis_index("pair")


def owner_of_left(t):
    return (t * N) // TL


def hops(step):
    return sum(min(s, n - s) for s, n in zip(step, (X, Y, PAIR)))


STEPS = sorted(
    ((x, y, z, c) for x in range(X) for y in range(Y) for z in range(PAIR) for c in range(CORES) if x or y or z or c),
    key=lambda step: (-hops(step), (step[0] + 2 * step[1] + 3 * step[2]) % 4, step),
)


def peers():
    dp, z = lax.axis_index("dp"), lax.axis_index("pair")
    x, y, c = dp // (Y * CORES), (dp // CORES) % Y, dp % CORES
    xs = [((x + i) % X) * (Y * CORES) for i in range(X)]
    ys = [((y + i) % Y) * CORES for i in range(Y)]
    zs = [(z + i) % PAIR for i in range(PAIR)]
    cs = [(c + i) % CORES for i in range(CORES)]
    xy = [[i + j for j in ys] for i in xs]
    return [(xy[i][j] + cs[m], zs[k]) for i, j, k, m in STEPS]


def nearest(i):
    return (i * (i + 1) // 2) % X


def place():
    dp, z = lax.axis_index("dp"), lax.axis_index("pair")
    return dp // (Y * CORES), (dp // CORES) % Y, z, dp % CORES


def chip_device(chip, core):
    return ((chip // PAIR) * CORES + core, chip % PAIR)


def same_core_peers(i):
    x, y, z, c = place()
    base = ((x + X - nearest(i)) % X) * (Y * CORES) + c
    out = []
    for k, j in ((k, j) for k in (2, 1, 3, 0) for j in (2, 1, 3, 0)):
        if i or k or j:
            out.append((base + ((y + j) % Y) * CORES, (z + k) % PAIR))
    return out


def split(x):
    high = x.astype(BF16)
    rest = x - high.astype(F32)
    mid = rest.astype(BF16)
    low = (rest - mid.astype(F32)).astype(BF16)
    return high, mid, low


def put_parts(ref, columns, x):
    for i, part in enumerate(split(x)):
        ref[i * RANK:(i + 1) * RANK, columns] = part


def add_parts(acc):
    return (acc[2 * RANK:3 * RANK] + acc[RANK:2 * RANK]) + acc[0:RANK]


def lane_group(shape):
    return lax.broadcasted_iota(jnp.int32, shape, 1) // RANK


def regroup(tiles, to):
    group = lane_group((8, 128))
    out = None
    for q, tile in enumerate(tiles):
        moved = pltpu.roll(tile, (RANK * (q - to)) % 128, 1) if q != to else tile
        out = moved if out is None else jnp.where(group == q, moved, out)
    return out


def inverse_factor(parts_ref):
    gram = lax.dot_general(parts_ref[0:PARTS * RANK, :], parts_ref[...], NT, preferred_element_type=F32)
    gram = add_parts(gram)
    gram = (pltpu.roll(gram, 64, 1) + pltpu.roll(gram, 96, 1)) + gram
    lane = lax.broadcasted_iota(jnp.int32, (RANK, 128), 1)
    row = lax.broadcasted_iota(jnp.int32, (RANK, 128), 0)
    both = jnp.where(lane < RANK, gram, jnp.where(lane == row + RANK, 1.0, 0.0))
    for k in range(RANK - 1):
        pivot_row = both[k:k + 1, :]
        scaled = pivot_row / both[k:k + 1, k:k + 1]
        factor = jnp.where(row > k, jnp.broadcast_to(both[:, k:k + 1], (RANK, 128)), 0.0)
        both = both - factor * scaled
    pivots = jnp.sum(jnp.where(lane == row, both, 0.0), axis=1, keepdims=True)
    return (pltpu.roll(both, 96, 1) / jnp.sqrt(pivots))[:, 0:RANK]


def total(ref):
    sums = [jnp.sum(ref[i * 16:(i + 1) * 16], axis=0) for i in range(ref.shape[0] // 16)]
    while len(sums) > 1:
        sums = [a + b for a, b in zip(sums[::2], sums[1::2])]
    return sums[0] * SCALE


def wait_tiles(ref, count, sem):
    pltpu.make_async_copy(ref.at[pl.ds(0, count)], ref.at[pl.ds(0, count)], sem).wait()


def kernel(
    grads, errors, start, out,
    g, e, q, b_parts, l_parts, l_send, l_recv, l_all, r_send, r_pair, r_half, r_recv, r_all, tile, left,
    load_sem, send_sem, recv_sem, pair_send, pair_recv,
):
    me = position()
    my_x, my_y, my_z, core = place()
    my_chip = (my_x * Y + my_y) * PAIR + my_z
    partner = chip_device(my_chip, 1 - core)
    my_left = (me * TL + N - 1) // N
    owns_left = jnp.logical_and(my_left < TL, owner_of_left(my_left) == me)
    chunks = D // ROWS
    first_chunk = (me * chunks) // N + chunks // 2

    def load(i):
        rows = pl.ds(pl.multiple_of(((first_chunk + i) % chunks) * ROWS, ROWS), ROWS)
        return (
            pltpu.make_async_copy(grads.at[0, rows, :], g.at[rows, :], load_sem.at[i]),
            pltpu.make_async_copy(errors.at[0, rows, :], e.at[rows, :], load_sem.at[chunks + i]),
        )

    q_copy = pltpu.make_async_copy(start, q, load_sem.at[2 * chunks])
    q_copy.start()
    for i in range(chunks):
        for copy in load(i):
            copy.start()

    barrier = pltpu.get_barrier_semaphore()

    def greet(k, carry):
        pl.semaphore_signal(barrier, inc=1, device_id=device((me + k) % N), device_id_type=MESH)
        return carry

    lax.fori_loop(1, N, greet, 0)

    b_parts[PARTS * RANK:, :] = jnp.zeros((128 - PARTS * RANK, FF), BF16)
    l_parts[PARTS * RANK:, :] = jnp.zeros((128 - PARTS * RANK, D), BF16)
    left[:, D:] = jnp.zeros((RANK, 128), F32)
    q_copy.wait()

    def turn(j, carry):
        rows = pl.ds(pl.multiple_of(j * 128, 128), 128)
        put_parts(b_parts, rows, q[:, rows])
        return carry

    lax.fori_loop(0, FF // 128, turn, 0)

    def to_left_owner(it, t):
        owner = owner_of_left(t)

        @pl.when(owner != me)
        def _():
            pltpu.make_async_remote_copy(
                l_send.at[it, t], l_recv.at[it, me], send_sem.at[2 * it], recv_sem.at[2 * it],
                device_id=device(owner), device_id_type=MESH,
            ).start()

        @pl.when(owner == me)
        def _():
            l_recv[it, me] = l_send[it, t]

    def send_left(it, chunk, size, acc):
        tiles = size // 128 * GROUPS
        for j in range(tiles):
            lanes = slice(j // GROUPS * 128, j // GROUPS * 128 + 128)
            ranks = slice(j % GROUPS * 8, j % GROUPS * 8 + 8)
            l_send[it, chunk * tiles + j] = acc[ranks, lanes]

        def send(j, carry):
            to_left_owner(it, chunk * tiles + j)
            return carry

        lax.fori_loop(0, tiles, send, 0)

    def left_chunk(i):
        chunk = (first_chunk + i) % chunks
        rows = pl.ds(pl.multiple_of(chunk * ROWS, ROWS), ROWS)
        parts = b_parts[0:PARTS * RANK, :]
        acc = lax.dot_general(parts, g[rows, :], NT, preferred_element_type=F32)
        acc = acc + lax.dot_general(parts, e[rows, :], NT, preferred_element_type=F32)
        send_left(0, chunk, ROWS, add_parts(acc))

    def right_chunk(it, i):
        x = (my_x + nearest(STEPS_X - 1 - i)) % X
        columns = pl.ds(pl.multiple_of(x * COLS, COLS), COLS)
        parts = l_parts[0:PARTS * RANK, :]
        acc = jnp.dot(parts, g[:, columns], preferred_element_type=F32)
        acc = acc + jnp.dot(parts, e[:, columns], preferred_element_type=F32)
        acc = add_parts(acc)
        for j in range(COLS // 128):
            tiles = [acc[r * 8:r * 8 + 8, j * 128:j * 128 + 128] for r in range(GROUPS)]
            for r in range(PAIR):
                r_send[it, j % CORES, x * PLANE + j // CORES * PAIR + r] = regroup(tiles, r)
        chips = pl.ds(x * PLANE, PLANE)
        pltpu.make_async_remote_copy(
            r_send.at[it, 1 - core, chips], r_pair.at[it, chips], pair_send.at[it], pair_recv.at[it, i],
            device_id=partner, device_id_type=MESH,
        ).start()

    def right_pair(it, i):
        x = (my_x + nearest(STEPS_X - 1 - i)) % X
        chips = pl.ds(x * PLANE, PLANE)
        wait_tiles(r_pair.at[it, chips], PLANE, pair_recv.at[it, i])
        r_half[it, chips] = r_send[it, core, chips] + r_pair[it, chips]

        def send(j, carry):
            chip = x * PLANE + j

            @pl.when(chip != my_chip)
            def _():
                pltpu.make_async_remote_copy(
                    r_half.at[it, chip], r_recv.at[it, my_chip], send_sem.at[2 * it + 1], recv_sem.at[2 * it + 1],
                    device_id=chip_device(chip, core), device_id_type=MESH,
                ).start()

            @pl.when(chip == my_chip)
            def _():
                r_recv[it, my_chip] = r_half[it, chip]

            return carry

        lax.fori_loop(0, PLANE, send, 0)

    def right_product(it):
        def step(i, carry):
            right_chunk(it, i)

            @pl.when(i > 0)
            def _():
                right_pair(it, i - 1)

            return carry

        lax.fori_loop(0, STEPS_X, step, 0)
        right_pair(it, STEPS_X - 1)

    def send_left_sums(it):
        @pl.when(owns_left)
        def _():
            wait_tiles(l_recv.at[it], N - 1, recv_sem.at[2 * it])
            tile[it] = total(l_recv.at[it])

            for peer in peers():
                pltpu.make_async_remote_copy(
                    tile.at[it], l_all.at[it, my_left], send_sem.at[4 + it], recv_sem.at[4 + it],
                    device_id=peer, device_id_type=MESH,
                ).start()
            l_all[it, my_left] = tile[it]
            wait_tiles(l_all.at[it], TL - 1, recv_sem.at[4 + it])

        @pl.when(jnp.logical_not(owns_left))
        def _():
            wait_tiles(l_all.at[it], TL, recv_sem.at[4 + it])

    def right_sum(it, inverse):
        wait_tiles(r_recv.at[it], CHIPS - 1, recv_sem.at[2 * it + 1])
        summed = total(r_recv.at[it])
        ranks = [pltpu.roll(summed, (128 - RANK * r) % 128, 1) if r else summed for r in range(GROUPS)]
        return jnp.dot(inverse, jnp.concatenate(ranks, axis=0), precision=EXACT, preferred_element_type=F32)

    for i in range(chunks):
        for copy in load(i):
            copy.wait()
        if i == 0:
            pl.semaphore_wait(barrier, N - 1)
        left_chunk(i)
    send_left_sums(0)
    for j in range(D // 128):
        block = jnp.concatenate([l_all[0, j * GROUPS + r] for r in range(GROUPS)], axis=0)
        put_parts(l_parts, slice(j * 128, j * 128 + 128), block)
    right_product(0)
    inverse = inverse_factor(l_parts)
    mine = right_sum(0, inverse)
    packed = mine[0:8]
    group = lane_group((8, 128))
    for r in range(1, GROUPS):
        packed = jnp.where(group == r, pltpu.roll(mine[r * 8:r * 8 + 8], RANK * r, 1), packed)
    tile[2] = packed

    r_all[core, my_chip] = tile[2]

    def send_right(i):
        for peer in same_core_peers(i):
            pltpu.make_async_remote_copy(
                tile.at[2], r_all.at[core, my_chip], send_sem.at[6], recv_sem.at[6 + my_x],
                device_id=peer, device_id_type=MESH,
            ).start()

    def plane(i):
        return (my_x + nearest(i)) % X

    def pass_on(i):
        chips = pl.ds(plane(i) * PLANE, PLANE)
        tiles = r_all.at[core, chips]
        wait_tiles(tiles, PLANE - 1 if i == 0 else PLANE, recv_sem.at[6 + plane(i)])
        pltpu.make_async_remote_copy(
            tiles, tiles, pair_send.at[2], pair_recv.at[2, i], device_id=partner, device_id_type=MESH
        ).start()

    def unpack(i):
        chips = pl.ds(plane(i) * PLANE, PLANE)
        wait_tiles(r_all.at[1 - core, chips], PLANE, pair_recv.at[2, i])
        for j in range(COLS // 128):
            four = [r_all[j % CORES, plane(i) * PLANE + j // CORES * PAIR + r] for r in range(PAIR)]
            block = jnp.concatenate([regroup(four, r) for r in range(GROUPS)], axis=0)
            put_parts(b_parts, slice(i * COLS + j * 128, i * COLS + j * 128 + 128), block)

    def some_columns(i, rows):
        columns = pl.ds(pl.multiple_of(plane(i) * COLS, COLS), COLS)
        parts = b_parts[0:PARTS * RANK, i * COLS:i * COLS + COLS]
        acc = lax.dot_general(parts, g[rows, columns], NT, preferred_element_type=F32)
        acc = acc + lax.dot_general(parts, e[rows, columns], NT, preferred_element_type=F32)
        return add_parts(acc)

    def columns_step(i, r):
        rows = slice(r, r + ROWS2)
        if i == 0:
            left[:, rows] = some_columns(i, rows)
        else:
            left[:, rows] += some_columns(i, rows)

    for i in range(STEPS_X - 1):
        send_right(i)
    pass_on(0)
    send_right(STEPS_X - 1)
    unpack(0)
    for i in range(STEPS_X - 1):
        pass_on(i + 1)
        columns_step(i, 0)
        unpack(i + 1)
        for r in range(ROWS2, D, ROWS2):
            columns_step(i, r)

    def last_columns(i, carry):
        steps = D // ROWS2
        chunk = ((me * steps) // N + steps // 2 + i) % steps
        rows = pl.ds(pl.multiple_of(chunk * ROWS2, ROWS2), ROWS2)
        send_left(1, chunk, ROWS2, left[:, rows] + some_columns(STEPS_X - 1, rows))
        return carry

    lax.fori_loop(0, D // ROWS2, last_columns, 0)
    inverse = inverse_factor(b_parts)
    send_left_sums(1)
    for j in range(D // 512):
        block = jnp.concatenate(
            [
                jnp.concatenate([l_all[1, (j * 4 + i) * GROUPS + r] for r in range(GROUPS)], axis=0)
                for i in range(4)
            ],
            axis=1,
        )
        block = jnp.dot(inverse, block, precision=EXACT, preferred_element_type=F32)
        left[:, j * 512:j * 512 + 512] = block
        put_parts(l_parts, slice(j * 512, j * 512 + 512), block)
    right_product(1)
    at = (me * OUT_L) // 128
    block = left[:, pl.ds(pl.multiple_of(at * 128, 128), 256)]
    block = pltpu.roll(block, (256 - (me * OUT_L - at * 128)) % 256, 1)[:, 0:128]
    out[0:OUT_L, :] = block.T[0:OUT_L, :]
    inverse = inverse_factor(l_parts)
    mine = right_sum(1, inverse)
    out[OUT_AT:OUT_AT + OUT_R, :] = mine.T[0:OUT_R, :]

    for it in range(2):
        @pl.when(owns_left)
        def _():
            wait_tiles(l_send.at[it], TL - 1, send_sem.at[2 * it])
            wait_tiles(l_recv.at[it], N - 1, send_sem.at[4 + it])

        @pl.when(jnp.logical_not(owns_left))
        def _():
            wait_tiles(l_send.at[it], TL, send_sem.at[2 * it])

        wait_tiles(r_half.at[it], CHIPS - 1, send_sem.at[2 * it + 1])
        wait_tiles(r_pair.at[it], CHIPS, pair_send.at[it])
    wait_tiles(r_all.at[0], CHIPS - 1, send_sem.at[6])
    wait_tiles(r_all.at[0], CHIPS, pair_send.at[2])


def shards(local_grads, error_feedback, q_start):
    anywhere = pl.BlockSpec(memory_space=pl.ANY)
    vmem = pl.BlockSpec(memory_space=pltpu.VMEM)
    out = pl.pallas_call(
        kernel,
        out_shape=jax.ShapeDtypeStruct((OUT_AT + OUT_R, RANK), F32),
        in_specs=[anywhere, anywhere, anywhere],
        out_specs=vmem,
        scratch_shapes=[
            pltpu.VMEM((D, FF), BF16),
            pltpu.VMEM((D, FF), BF16),
            pltpu.VMEM((RANK, FF), F32),
            pltpu.VMEM((128, FF), BF16),
            pltpu.VMEM((128, D), BF16),
            pltpu.VMEM((2, TL, 8, 128), F32),
            pltpu.VMEM((2, N, 8, 128), F32),
            pltpu.VMEM((2, TL, 8, 128), F32),
            pltpu.VMEM((2, CORES, CHIPS, 8, 128), F32),
            pltpu.VMEM((2, CHIPS, 8, 128), F32),
            pltpu.VMEM((2, CHIPS, 8, 128), F32),
            pltpu.VMEM((2, CHIPS, 8, 128), F32),
            pltpu.VMEM((CORES, CHIPS, 8, 128), F32),
            pltpu.VMEM((3, 8, 128), F32),
            pltpu.VMEM((RANK, D + 128), F32),
            pltpu.SemaphoreType.DMA((2 * (D // ROWS) + 1,)),
            pltpu.SemaphoreType.DMA((7,)),
            pltpu.SemaphoreType.DMA((6 + X,)),
            pltpu.SemaphoreType.DMA((3,)),
            pltpu.SemaphoreType.DMA((3, STEPS_X)),
        ],
        compiler_params=pltpu.CompilerParams(
            vmem_limit_bytes=60 << 20, collective_id=0, has_side_effects=True
        ),
    )(local_grads, error_feedback, q_start.T)
    return (out[0:OUT_L], out[OUT_AT:OUT_AT + OUT_R])


def solution(mesh):
    return jax.shard_map(
        shards,
        mesh=mesh,
        in_specs=(P(("dp", "pair"), None, None), P(("dp", "pair"), None, None), P()),
        out_specs=(P(("dp", "pair"), None), P(("dp", "pair"), None)),
        check_vma=False,
    )
```

```python
import functools

import jax
import jax.numpy as jnp
from jax import lax
from jax.experimental import pallas as pl
from jax.experimental.pallas import tpu as pltpu
from jax.sharding import PartitionSpec as P

MESH = pl.DeviceIdType.MESH
F32 = jnp.float32
BF16 = jnp.bfloat16
EXACT = lax.Precision.HIGHEST

X, Y, CORES, PAIR = 4, 4, 2, 4
N = X * Y * CORES * PAIR
D, FF, RANK = 1536, 4096, 32
PARTS = 3
GROUPS = RANK // 8
TL = D // 128 * GROUPS
ROWS = 512
COLS = 1024
ROWS2 = 512
STEPS_X = FF // COLS
CHIPS = N // CORES
PLANE = CHIPS // X
SCALE = 1.0 / N
OUT_L, OUT_R = D // N, FF // N
OUT_AT = -(-OUT_L // 8) * 8

NT = (((1,), (1,)), ((), ()))


def device(i):
    return (i // PAIR, i % PAIR)


def position():
    return lax.axis_index("dp") * PAIR + lax.axis_index("pair")


def owner_of_left(t):
    return (t * N) // TL


def hops(step):
    return sum(min(s, n - s) for s, n in zip(step, (X, Y, PAIR)))


STEPS = sorted(
    ((x, y, z, c) for x in range(X) for y in range(Y) for z in range(PAIR) for c in range(CORES) if x or y or z or c),
    key=lambda step: (-hops(step), (step[0] + 2 * step[1] + 3 * step[2]) % 4, step),
)


def peers():
    dp, z = lax.axis_index("dp"), lax.axis_index("pair")
    x, y, c = dp // (Y * CORES), (dp // CORES) % Y, dp % CORES
    xs = [((x + i) % X) * (Y * CORES) for i in range(X)]
    ys = [((y + i) % Y) * CORES for i in range(Y)]
    zs = [(z + i) % PAIR for i in range(PAIR)]
    cs = [(c + i) % CORES for i in range(CORES)]
    xy = [[i + j for j in ys] for i in xs]
    return [(xy[i][j] + cs[m], zs[k]) for i, j, k, m in STEPS]


def nearest(i):
    return (i * (i + 1) // 2) % X


def place():
    dp, z = lax.axis_index("dp"), lax.axis_index("pair")
    return dp // (Y * CORES), (dp // CORES) % Y, z, dp % CORES


def chip_device(chip, core):
    return ((chip // PAIR) * CORES + core, chip % PAIR)


def same_core_peers(i):
    x, y, z, c = place()
    base = ((x + X - nearest(i)) % X) * (Y * CORES) + c
    out = []
    for k, j in ((k, j) for k in (2, 1, 3, 0) for j in (2, 1, 3, 0)):
        if i or k or j:
            out.append((base + ((y + j) % Y) * CORES, (z + k) % PAIR))
    return out


def split(x):
    high = x.astype(BF16)
    rest = x - high.astype(F32)
    mid = rest.astype(BF16)
    low = (rest - mid.astype(F32)).astype(BF16)
    return high, mid, low


def put_parts(ref, columns, x):
    for i, part in enumerate(split(x)):
        ref[i * RANK:(i + 1) * RANK, columns] = part


def add_parts(acc):
    return (acc[2 * RANK:3 * RANK] + acc[RANK:2 * RANK]) + acc[0:RANK]


def lane_group(shape):
    return lax.broadcasted_iota(jnp.int32, shape, 1) // RANK


def regroup(tiles, to):
    group = lane_group((8, 128))
    out = None
    for q, tile in enumerate(tiles):
        moved = pltpu.roll(tile, (RANK * (q - to)) % 128, 1) if q != to else tile
        out = moved if out is None else jnp.where(group == q, moved, out)
    return out


def inverse_factor(parts_ref):
    gram = lax.dot_general(parts_ref[0:PARTS * RANK, :], parts_ref[...], NT, preferred_element_type=F32)
    gram = add_parts(gram)
    gram = (pltpu.roll(gram, 64, 1) + pltpu.roll(gram, 96, 1)) + gram
    lane = lax.broadcasted_iota(jnp.int32, (RANK, 128), 1)
    row = lax.broadcasted_iota(jnp.int32, (RANK, 128), 0)
    both = jnp.where(lane < RANK, gram, jnp.where(lane == row + RANK, 1.0, 0.0))
    for k in range(RANK - 1):
        pivot_row = both[k:k + 1, :]
        scaled = pivot_row / both[k:k + 1, k:k + 1]
        factor = jnp.where(row > k, jnp.broadcast_to(both[:, k:k + 1], (RANK, 128)), 0.0)
        both = both - factor * scaled
    pivots = jnp.sum(jnp.where(lane == row, both, 0.0), axis=1, keepdims=True)
    return (pltpu.roll(both, 96, 1) / jnp.sqrt(pivots))[:, 0:RANK]


def total(ref):
    sums = [jnp.sum(ref[i * 16:(i + 1) * 16], axis=0) for i in range(ref.shape[0] // 16)]
    while len(sums) > 1:
        sums = [a + b for a, b in zip(sums[::2], sums[1::2])]
    return sums[0] * SCALE


def wait_tiles(ref, count, sem):
    pltpu.make_async_copy(ref.at[pl.ds(0, count)], ref.at[pl.ds(0, count)], sem).wait()


def kernel(
    grads, errors, start, out,
    g, e, q, b_parts, l_parts, l_send, l_recv, l_all, r_send, r_pair, r_half, r_recv, r_all, tile, left,
    load_sem, send_sem, recv_sem, pair_send, pair_recv,
):
    me = position()
    my_x, my_y, my_z, core = place()
    my_chip = (my_x * Y + my_y) * PAIR + my_z
    partner = chip_device(my_chip, 1 - core)
    my_left = (me * TL + N - 1) // N
    owns_left = jnp.logical_and(my_left < TL, owner_of_left(my_left) == me)
    chunks = D // ROWS
    first_chunk = (me * chunks) // N + chunks // 2

    def load(i):
        rows = pl.ds(pl.multiple_of(((first_chunk + i) % chunks) * ROWS, ROWS), ROWS)
        return (
            pltpu.make_async_copy(grads.at[0, rows, :], g.at[rows, :], load_sem.at[i]),
            pltpu.make_async_copy(errors.at[0, rows, :], e.at[rows, :], load_sem.at[chunks + i]),
        )

    q_copy = pltpu.make_async_copy(start, q, load_sem.at[2 * chunks])
    q_copy.start()
    for i in range(chunks):
        for copy in load(i):
            copy.start()

    barrier = pltpu.get_barrier_semaphore()

    def greet(k, carry):
        pl.semaphore_signal(barrier, inc=1, device_id=device((me + k) % N), device_id_type=MESH)
        return carry

    lax.fori_loop(1, N, greet, 0)

    b_parts[PARTS * RANK:, :] = jnp.zeros((128 - PARTS * RANK, FF), BF16)
    l_parts[PARTS * RANK:, :] = jnp.zeros((128 - PARTS * RANK, D), BF16)
    left[:, D:] = jnp.zeros((RANK, 128), F32)
    q_copy.wait()

    def turn(j, carry):
        rows = pl.ds(pl.multiple_of(j * 128, 128), 128)
        put_parts(b_parts, rows, q[:, rows])
        return carry

    lax.fori_loop(0, FF // 128, turn, 0)

    def to_left_owner(it, t):
        owner = owner_of_left(t)

        @pl.when(owner != me)
        def _():
            pltpu.make_async_remote_copy(
                l_send.at[it, t], l_recv.at[it, me], send_sem.at[2 * it], recv_sem.at[2 * it],
                device_id=device(owner), device_id_type=MESH,
            ).start()

        @pl.when(owner == me)
        def _():
            l_recv[it, me] = l_send[it, t]

    def put_left(it, chunk, size, acc):
        tiles = size // 128 * GROUPS
        for j in range(tiles):
            lanes = slice(j // GROUPS * 128, j // GROUPS * 128 + 128)
            ranks = slice(j % GROUPS * 8, j % GROUPS * 8 + 8)
            l_send[it, chunk * tiles + j] = acc[ranks, lanes]

    def send_left(it, chunk, size):
        tiles = size // 128 * GROUPS

        for j in range(tiles):
            to_left_owner(it, chunk * tiles + j)

    def left_chunk(i):
        chunk = (first_chunk + i) % chunks
        rows = pl.ds(pl.multiple_of(chunk * ROWS, ROWS), ROWS)
        parts = b_parts[0:PARTS * RANK, :]
        acc = lax.dot_general(parts, g[rows, :], NT, preferred_element_type=F32)
        acc = acc + lax.dot_general(parts, e[rows, :], NT, preferred_element_type=F32)
        put_left(0, chunk, ROWS, add_parts(acc))

    def right_chunk(it, i):
        x = (my_x + nearest(STEPS_X - 1 - i)) % X
        columns = pl.ds(pl.multiple_of(x * COLS, COLS), COLS)
        parts = l_parts[0:PARTS * RANK, :]
        acc = jnp.dot(parts, g[:, columns], preferred_element_type=F32)
        acc = acc + jnp.dot(parts, e[:, columns], preferred_element_type=F32)
        acc = add_parts(acc)
        for j in range(COLS // 128):
            tiles = [acc[r * 8:r * 8 + 8, j * 128:j * 128 + 128] for r in range(GROUPS)]
            for r in range(PAIR):
                r_send[it, j % CORES, x * PLANE + j // CORES * PAIR + r] = regroup(tiles, r)
        chips = pl.ds(x * PLANE, PLANE)
        pltpu.make_async_remote_copy(
            r_send.at[it, 1 - core, chips], r_pair.at[it, chips], pair_send.at[it], pair_recv.at[it, i],
            device_id=partner, device_id_type=MESH,
        ).start()

    def right_pair(it, i, own):
        x = (my_x + nearest(STEPS_X - 1 - i)) % X
        chips = pl.ds(x * PLANE, PLANE)
        wait_tiles(r_pair.at[it, chips], PLANE, pair_recv.at[it, i])
        r_half[it, chips] = r_send[it, core, chips] + r_pair[it, chips]

        def send(chip):
            pltpu.make_async_remote_copy(
                r_half.at[it, chip], r_recv.at[it, my_chip], send_sem.at[2 * it + 1], recv_sem.at[2 * it + 1],
                device_id=chip_device(chip, core), device_id_type=MESH,
            ).start()

        for j in range(PLANE):
            chip = x * PLANE + j
            if not own:
                send(chip)
                continue

            pl.when(chip != my_chip)(functools.partial(send, chip))

        if own:
            r_recv[it, my_chip] = r_half[it, my_chip]

    def right_product(it):
        def step(i, carry):
            right_chunk(it, i)

            @pl.when(i > 0)
            def _():
                right_pair(it, i - 1, False)

            return carry

        lax.fori_loop(0, STEPS_X, step, 0)
        right_pair(it, STEPS_X - 1, True)

    def send_left_sums(it):
        @pl.when(owns_left)
        def _():
            wait_tiles(l_recv.at[it], N - 1, recv_sem.at[2 * it])
            tile[it] = total(l_recv.at[it])

            for peer in peers():
                pltpu.make_async_remote_copy(
                    tile.at[it], l_all.at[it, my_left], send_sem.at[4 + it], recv_sem.at[4 + it],
                    device_id=peer, device_id_type=MESH,
                ).start()
            l_all[it, my_left] = tile[it]
            wait_tiles(l_all.at[it], TL - 1, recv_sem.at[4 + it])

        @pl.when(jnp.logical_not(owns_left))
        def _():
            wait_tiles(l_all.at[it], TL, recv_sem.at[4 + it])

    def right_sum(it, inverse):
        wait_tiles(r_recv.at[it], CHIPS - 1, recv_sem.at[2 * it + 1])
        summed = total(r_recv.at[it])
        ranks = [pltpu.roll(summed, (128 - RANK * r) % 128, 1) if r else summed for r in range(GROUPS)]
        return jnp.dot(inverse, jnp.concatenate(ranks, axis=0), precision=EXACT, preferred_element_type=F32)

    for i in range(chunks):
        for copy in load(i):
            copy.wait()
        left_chunk(i)
        if i == 1:
            pl.semaphore_wait(barrier, N - 1)
            send_left(0, first_chunk % chunks, ROWS)
        if i >= 1:
            send_left(0, (first_chunk + i) % chunks, ROWS)
    send_left_sums(0)
    for j in range(D // 128):
        block = jnp.concatenate([l_all[0, j * GROUPS + r] for r in range(GROUPS)], axis=0)
        put_parts(l_parts, slice(j * 128, j * 128 + 128), block)
    right_product(0)
    inverse = inverse_factor(l_parts)
    mine = right_sum(0, inverse)
    packed = mine[0:8]
    group = lane_group((8, 128))
    for r in range(1, GROUPS):
        packed = jnp.where(group == r, pltpu.roll(mine[r * 8:r * 8 + 8], RANK * r, 1), packed)
    tile[2] = packed

    r_all[core, my_chip] = tile[2]

    def send_right(i):
        for peer in same_core_peers(i):
            pltpu.make_async_remote_copy(
                tile.at[2], r_all.at[core, my_chip], send_sem.at[6], recv_sem.at[6 + my_x],
                device_id=peer, device_id_type=MESH,
            ).start()

    def plane(i):
        return (my_x + nearest(i)) % X

    def pass_on(i):
        chips = pl.ds(plane(i) * PLANE, PLANE)
        tiles = r_all.at[core, chips]
        wait_tiles(tiles, PLANE - 1 if i == 0 else PLANE, recv_sem.at[6 + plane(i)])
        pltpu.make_async_remote_copy(
            tiles, tiles, pair_send.at[2], pair_recv.at[2, i], device_id=partner, device_id_type=MESH
        ).start()

    def unpack(i):
        chips = pl.ds(plane(i) * PLANE, PLANE)
        wait_tiles(r_all.at[1 - core, chips], PLANE, pair_recv.at[2, i])
        for j in range(COLS // 128):
            four = [r_all[j % CORES, plane(i) * PLANE + j // CORES * PAIR + r] for r in range(PAIR)]
            block = jnp.concatenate([regroup(four, r) for r in range(GROUPS)], axis=0)
            put_parts(b_parts, slice(i * COLS + j * 128, i * COLS + j * 128 + 128), block)

    def some_columns(i, rows):
        columns = pl.ds(pl.multiple_of(plane(i) * COLS, COLS), COLS)
        parts = b_parts[0:PARTS * RANK, i * COLS:i * COLS + COLS]
        acc = lax.dot_general(parts, g[rows, columns], NT, preferred_element_type=F32)
        acc = acc + lax.dot_general(parts, e[rows, columns], NT, preferred_element_type=F32)
        return add_parts(acc)

    def columns_step(i, r):
        rows = slice(r, r + ROWS2)
        if i == 0:
            left[:, rows] = some_columns(i, rows)
        else:
            left[:, rows] += some_columns(i, rows)

    for i in range(STEPS_X - 1):
        send_right(i)
    pass_on(0)
    send_right(STEPS_X - 1)
    unpack(0)
    for i in range(STEPS_X - 1):
        pass_on(i + 1)
        columns_step(i, 0)
        unpack(i + 1)
        for r in range(ROWS2, D, ROWS2):
            columns_step(i, r)

    def last_columns(i, carry):
        steps = D // ROWS2
        chunk = ((me * steps) // N + steps // 2 + i) % steps
        rows = pl.ds(pl.multiple_of(chunk * ROWS2, ROWS2), ROWS2)
        put_left(1, chunk, ROWS2, left[:, rows] + some_columns(STEPS_X - 1, rows))
        send_left(1, chunk, ROWS2)
        return carry

    lax.fori_loop(0, D // ROWS2, last_columns, 0)
    inverse = inverse_factor(b_parts)
    send_left_sums(1)
    for j in range(D // 512):
        block = jnp.concatenate(
            [
                jnp.concatenate([l_all[1, (j * 4 + i) * GROUPS + r] for r in range(GROUPS)], axis=0)
                for i in range(4)
            ],
            axis=1,
        )
        block = jnp.dot(inverse, block, precision=EXACT, preferred_element_type=F32)
        left[:, j * 512:j * 512 + 512] = block
        put_parts(l_parts, slice(j * 512, j * 512 + 512), block)
    right_product(1)
    at = (me * OUT_L) // 128
    block = left[:, pl.ds(pl.multiple_of(at * 128, 128), 256)]
    block = pltpu.roll(block, (256 - (me * OUT_L - at * 128)) % 256, 1)[:, 0:128]
    out[0:OUT_L, :] = block.T[0:OUT_L, :]
    inverse = inverse_factor(l_parts)
    mine = right_sum(1, inverse)
    out[OUT_AT:OUT_AT + OUT_R, :] = mine.T[0:OUT_R, :]

    for it in range(2):
        @pl.when(owns_left)
        def _():
            wait_tiles(l_send.at[it], TL - 1, send_sem.at[2 * it])
            wait_tiles(l_recv.at[it], N - 1, send_sem.at[4 + it])

        @pl.when(jnp.logical_not(owns_left))
        def _():
            wait_tiles(l_send.at[it], TL, send_sem.at[2 * it])

        wait_tiles(r_half.at[it], CHIPS - 1, send_sem.at[2 * it + 1])
        wait_tiles(r_pair.at[it], CHIPS, pair_send.at[it])
    wait_tiles(r_all.at[0], CHIPS - 1, send_sem.at[6])
    wait_tiles(r_all.at[0], CHIPS, pair_send.at[2])


def hand_out(both, left, right):
    left[...] = both[0:OUT_L, :]
    right[...] = both[OUT_AT:OUT_AT + OUT_R, :]


def shards(local_grads, error_feedback, q_start):
    anywhere = pl.BlockSpec(memory_space=pl.ANY)
    vmem = pl.BlockSpec(memory_space=pltpu.VMEM)
    out = pl.pallas_call(
        kernel,
        out_shape=jax.ShapeDtypeStruct((OUT_AT + OUT_R, RANK), F32),
        in_specs=[anywhere, anywhere, anywhere],
        out_specs=vmem,
        scratch_shapes=[
            pltpu.VMEM((D, FF), BF16),
            pltpu.VMEM((D, FF), BF16),
            pltpu.VMEM((RANK, FF), F32),
            pltpu.VMEM((128, FF), BF16),
            pltpu.VMEM((128, D), BF16),
            pltpu.VMEM((2, TL, 8, 128), F32),
            pltpu.VMEM((2, N, 8, 128), F32),
            pltpu.VMEM((2, TL, 8, 128), F32),
            pltpu.VMEM((2, CORES, CHIPS, 8, 128), F32),
            pltpu.VMEM((2, CHIPS, 8, 128), F32),
            pltpu.VMEM((2, CHIPS, 8, 128), F32),
            pltpu.VMEM((2, CHIPS, 8, 128), F32),
            pltpu.VMEM((CORES, CHIPS, 8, 128), F32),
            pltpu.VMEM((3, 8, 128), F32),
            pltpu.VMEM((RANK, D + 128), F32),
            pltpu.SemaphoreType.DMA((2 * (D // ROWS) + 1,)),
            pltpu.SemaphoreType.DMA((7,)),
            pltpu.SemaphoreType.DMA((6 + X,)),
            pltpu.SemaphoreType.DMA((3,)),
            pltpu.SemaphoreType.DMA((3, STEPS_X)),
        ],
        compiler_params=pltpu.CompilerParams(
            vmem_limit_bytes=60 << 20, collective_id=0, has_side_effects=True
        ),
    )(local_grads, error_feedback, q_start.T)
    return pl.pallas_call(
        hand_out,
        out_shape=(
            jax.ShapeDtypeStruct((OUT_L, RANK), F32),
            jax.ShapeDtypeStruct((OUT_R, RANK), F32),
        ),
    )(out)


def solution(mesh):
    return jax.shard_map(
        shards,
        mesh=mesh,
        in_specs=(P(("dp", "pair"), None, None), P(("dp", "pair"), None, None), P()),
        out_specs=(P(("dp", "pair"), None), P(("dp", "pair"), None)),
        check_vma=False,
    )
```

```python
import functools

import jax
import jax.numpy as jnp
from jax import lax
from jax.experimental import pallas as pl
from jax.experimental.pallas import tpu as pltpu
from jax.sharding import PartitionSpec as P

MESH = pl.DeviceIdType.MESH
F32 = jnp.float32
BF16 = jnp.bfloat16
EXACT = lax.Precision.HIGHEST

X, Y, CORES, PAIR = 4, 4, 2, 4
N = X * Y * CORES * PAIR
D, FF, RANK = 1536, 4096, 32
PARTS = 3
GROUPS = RANK // 8
TL = D // 128 * GROUPS
ROWS = 512
COLS = 1024
ROWS2 = 512
STEPS_X = FF // COLS
CHIPS = N // CORES
PLANE = CHIPS // X
SCALE = 1.0 / N
OUT_L, OUT_R = D // N, FF // N
OUT_AT = -(-OUT_L // 8) * 8

NT = (((1,), (1,)), ((), ()))


def device(i):
    return (i // PAIR, i % PAIR)


def position():
    return lax.axis_index("dp") * PAIR + lax.axis_index("pair")


def owner_of_left(t):
    return (t * N) // TL


def hops(step):
    return sum(min(s, n - s) for s, n in zip(step, (X, Y, PAIR)))


STEPS = sorted(
    ((x, y, z, c) for x in range(X) for y in range(Y) for z in range(PAIR) for c in range(CORES) if x or y or z or c),
    key=lambda step: (-hops(step), (step[0] + 2 * step[1] + 3 * step[2]) % 4, step),
)


def peers():
    dp, z = lax.axis_index("dp"), lax.axis_index("pair")
    x, y, c = dp // (Y * CORES), (dp // CORES) % Y, dp % CORES
    xs = [((x + i) % X) * (Y * CORES) for i in range(X)]
    ys = [((y + i) % Y) * CORES for i in range(Y)]
    zs = [(z + i) % PAIR for i in range(PAIR)]
    cs = [(c + i) % CORES for i in range(CORES)]
    xy = [[i + j for j in ys] for i in xs]
    return [(xy[i][j] + cs[m], zs[k]) for i, j, k, m in STEPS]


def nearest(i):
    return (i * (i + 1) // 2) % X


def place():
    dp, z = lax.axis_index("dp"), lax.axis_index("pair")
    return dp // (Y * CORES), (dp // CORES) % Y, z, dp % CORES


def chip_device(chip, core):
    return ((chip // PAIR) * CORES + core, chip % PAIR)


def same_core_peers(i):
    x, y, z, c = place()
    base = ((x + X - nearest(i)) % X) * (Y * CORES) + c
    out = []
    for k, j in ((k, j) for k in (2, 1, 3, 0) for j in (2, 1, 3, 0)):
        if i or k or j:
            out.append((base + ((y + j) % Y) * CORES, (z + k) % PAIR))
    return out


def split(x):
    high = x.astype(BF16)
    rest = x - high.astype(F32)
    mid = rest.astype(BF16)
    low = (rest - mid.astype(F32)).astype(BF16)
    return high, mid, low


def put_parts(ref, columns, x):
    for i, part in enumerate(split(x)):
        ref[i * RANK:(i + 1) * RANK, columns] = part


def add_parts(acc):
    return (acc[2 * RANK:3 * RANK] + acc[RANK:2 * RANK]) + acc[0:RANK]


def lane_group(shape):
    return lax.broadcasted_iota(jnp.int32, shape, 1) // RANK


def regroup(tiles, to):
    group = lane_group((8, 128))
    out = None
    for q, tile in enumerate(tiles):
        moved = pltpu.roll(tile, (RANK * (q - to)) % 128, 1) if q != to else tile
        out = moved if out is None else jnp.where(group == q, moved, out)
    return out


def inverse_factor(parts_ref):
    gram = lax.dot_general(parts_ref[0:PARTS * RANK, :], parts_ref[...], NT, preferred_element_type=F32)
    gram = add_parts(gram)
    gram = (pltpu.roll(gram, 64, 1) + pltpu.roll(gram, 96, 1)) + gram
    lane = lax.broadcasted_iota(jnp.int32, (RANK, 128), 1)
    row = lax.broadcasted_iota(jnp.int32, (RANK, 128), 0)
    both = jnp.where(lane < RANK, gram, jnp.where(lane == row + RANK, 1.0, 0.0))
    for k in range(RANK - 1):
        pivot_row = both[k:k + 1, :]
        scaled = pivot_row / both[k:k + 1, k:k + 1]
        factor = jnp.where(row > k, jnp.broadcast_to(both[:, k:k + 1], (RANK, 128)), 0.0)
        both = both - factor * scaled
    pivots = jnp.sum(jnp.where(lane == row, both, 0.0), axis=1, keepdims=True)
    return (pltpu.roll(both, 96, 1) / jnp.sqrt(pivots))[:, 0:RANK]


def total(ref):
    sums = [jnp.sum(ref[i * 16:(i + 1) * 16], axis=0) for i in range(ref.shape[0] // 16)]
    while len(sums) > 1:
        sums = [a + b for a, b in zip(sums[::2], sums[1::2])]
    return sums[0] * SCALE


def wait_tiles(ref, count, sem):
    pltpu.make_async_copy(ref.at[pl.ds(0, count)], ref.at[pl.ds(0, count)], sem).wait()


def kernel(
    grads, errors, start, out,
    g, e, q, b_parts, l_parts, l_send, l_recv, l_all, r_send, r_pair, r_half, r_recv, r_all, tile, left,
    load_sem, send_sem, far_send, recv_sem, pair_send, pair_recv,
):
    me = position()
    my_x, my_y, my_z, core = place()
    my_chip = (my_x * Y + my_y) * PAIR + my_z
    partner = chip_device(my_chip, 1 - core)
    my_left = (me * TL + N - 1) // N
    owns_left = jnp.logical_and(my_left < TL, owner_of_left(my_left) == me)
    chunks = D // ROWS
    first_chunk = (me * chunks) // N + chunks // 2

    def load(i):
        rows = pl.ds(pl.multiple_of(((first_chunk + i) % chunks) * ROWS, ROWS), ROWS)
        return (
            pltpu.make_async_copy(grads.at[0, rows, :], g.at[rows, :], load_sem.at[i]),
            pltpu.make_async_copy(errors.at[0, rows, :], e.at[rows, :], load_sem.at[chunks + i]),
        )

    q_copy = pltpu.make_async_copy(start, q, load_sem.at[2 * chunks])
    q_copy.start()
    for i in range(chunks):
        for copy in load(i):
            copy.start()

    barrier = pltpu.get_barrier_semaphore()

    def greet(k, carry):
        pl.semaphore_signal(barrier, inc=1, device_id=device((me + k) % N), device_id_type=MESH)
        return carry

    lax.fori_loop(1, N, greet, 0)

    b_parts[PARTS * RANK:, :] = jnp.zeros((128 - PARTS * RANK, FF), BF16)
    l_parts[PARTS * RANK:, :] = jnp.zeros((128 - PARTS * RANK, D), BF16)
    left[:, D:] = jnp.zeros((RANK, 128), F32)
    q_copy.wait()

    def turn(j, carry):
        rows = pl.ds(pl.multiple_of(j * 128, 128), 128)
        put_parts(b_parts, rows, q[:, rows])
        return carry

    lax.fori_loop(0, FF // 128, turn, 0)

    def to_left_owner(it, t):
        owner = owner_of_left(t)

        @pl.when(owner != me)
        def _():
            pltpu.make_async_remote_copy(
                l_send.at[it, t], l_recv.at[it, me], send_sem.at[2 * it], recv_sem.at[2 * it],
                device_id=device(owner), device_id_type=MESH,
            ).start()

        @pl.when(owner == me)
        def _():
            l_recv[it, me] = l_send[it, t]

    def put_left(it, chunk, size, acc):
        tiles = size // 128 * GROUPS
        for j in range(tiles):
            lanes = slice(j // GROUPS * 128, j // GROUPS * 128 + 128)
            ranks = slice(j % GROUPS * 8, j % GROUPS * 8 + 8)
            l_send[it, chunk * tiles + j] = acc[ranks, lanes]

    def send_left(it, chunk, size):
        tiles = size // 128 * GROUPS

        for j in range(tiles):
            to_left_owner(it, chunk * tiles + j)

    def left_chunk(i):
        chunk = (first_chunk + i) % chunks
        rows = pl.ds(pl.multiple_of(chunk * ROWS, ROWS), ROWS)
        parts = b_parts[0:PARTS * RANK, :]
        acc = lax.dot_general(parts, g[rows, :], NT, preferred_element_type=F32)
        acc = acc + lax.dot_general(parts, e[rows, :], NT, preferred_element_type=F32)
        put_left(0, chunk, ROWS, add_parts(acc))

    def right_chunk(it, i):
        x = (my_x + nearest(STEPS_X - 1 - i)) % X
        columns = pl.ds(pl.multiple_of(x * COLS, COLS), COLS)
        parts = l_parts[0:PARTS * RANK, :]
        acc = jnp.dot(parts, g[:, columns], preferred_element_type=F32)
        acc = acc + jnp.dot(parts, e[:, columns], preferred_element_type=F32)
        acc = add_parts(acc)
        for j in range(COLS // 128):
            tiles = [acc[r * 8:r * 8 + 8, j * 128:j * 128 + 128] for r in range(GROUPS)]
            for r in range(PAIR):
                r_send[it, j % CORES, x * PLANE + j // CORES * PAIR + r] = regroup(tiles, r)
        chips = pl.ds(x * PLANE, PLANE)
        pltpu.make_async_remote_copy(
            r_send.at[it, 1 - core, chips], r_pair.at[it, chips], pair_send.at[it], pair_recv.at[it, i],
            device_id=partner, device_id_type=MESH,
        ).start()

    def right_pair(it, i, own):
        x = (my_x + nearest(STEPS_X - 1 - i)) % X
        chips = pl.ds(x * PLANE, PLANE)
        wait_tiles(r_pair.at[it, chips], PLANE, pair_recv.at[it, i])
        r_half[it, chips] = r_send[it, core, chips] + r_pair[it, chips]

        def send(chip):
            pltpu.make_async_remote_copy(
                r_half.at[it, chip], r_recv.at[it, my_chip], send_sem.at[2 * it + 1], recv_sem.at[2 * it + 1],
                device_id=chip_device(chip, core), device_id_type=MESH,
            ).start()

        for j in range(PLANE):
            chip = x * PLANE + j
            if not own:
                send(chip)
                continue

            pl.when(chip != my_chip)(functools.partial(send, chip))

        if own:
            r_recv[it, my_chip] = r_half[it, my_chip]

    def right_product(it):
        def step(i, carry):
            right_chunk(it, i)

            @pl.when(i > 0)
            def _():
                right_pair(it, i - 1, False)

            return carry

        lax.fori_loop(0, STEPS_X, step, 0)
        right_pair(it, STEPS_X - 1, True)

    def send_left_sums(it):
        @pl.when(owns_left)
        def _():
            wait_tiles(l_recv.at[it], N - 1, recv_sem.at[2 * it])
            tile[it] = total(l_recv.at[it])

            for peer in peers():
                pltpu.make_async_remote_copy(
                    tile.at[it], l_all.at[it, my_left], send_sem.at[4 + it], recv_sem.at[4 + it],
                    device_id=peer, device_id_type=MESH,
                ).start()
            l_all[it, my_left] = tile[it]
            wait_tiles(l_all.at[it], TL - 1, recv_sem.at[4 + it])

        @pl.when(jnp.logical_not(owns_left))
        def _():
            wait_tiles(l_all.at[it], TL, recv_sem.at[4 + it])

    def right_sum(it, inverse):
        wait_tiles(r_recv.at[it], CHIPS - 1, recv_sem.at[2 * it + 1])
        summed = total(r_recv.at[it])
        ranks = [pltpu.roll(summed, (128 - RANK * r) % 128, 1) if r else summed for r in range(GROUPS)]
        return jnp.dot(inverse, jnp.concatenate(ranks, axis=0), precision=EXACT, preferred_element_type=F32)

    for i in range(chunks):
        for copy in load(i):
            copy.wait()
        left_chunk(i)
        if i == 1:
            pl.semaphore_wait(barrier, N - 1)
            send_left(0, first_chunk % chunks, ROWS)
        if i >= 1:
            send_left(0, (first_chunk + i) % chunks, ROWS)
    send_left_sums(0)
    for j in range(D // 128):
        block = jnp.concatenate([l_all[0, j * GROUPS + r] for r in range(GROUPS)], axis=0)
        put_parts(l_parts, slice(j * 128, j * 128 + 128), block)
    right_product(0)
    inverse = inverse_factor(l_parts)
    mine = right_sum(0, inverse)
    packed = mine[0:8]
    group = lane_group((8, 128))
    for r in range(1, GROUPS):
        packed = jnp.where(group == r, pltpu.roll(mine[r * 8:r * 8 + 8], RANK * r, 1), packed)
    tile[2] = packed

    r_all[core, my_chip] = tile[2]

    def send_right(i):
        for peer in same_core_peers(i):
            pltpu.make_async_remote_copy(
                tile.at[2], r_all.at[core, my_chip], send_sem.at[6] if i < 2 else far_send, recv_sem.at[6 + my_x],
                device_id=peer, device_id_type=MESH,
            ).start()

    def plane(i):
        return (my_x + nearest(i)) % X

    def pass_on(i):
        chips = pl.ds(plane(i) * PLANE, PLANE)
        tiles = r_all.at[core, chips]
        wait_tiles(tiles, PLANE - 1 if i == 0 else PLANE, recv_sem.at[6 + plane(i)])
        pltpu.make_async_remote_copy(
            tiles, tiles, pair_send.at[2], pair_recv.at[2, i], device_id=partner, device_id_type=MESH
        ).start()

    def unpack(i):
        chips = pl.ds(plane(i) * PLANE, PLANE)
        wait_tiles(r_all.at[1 - core, chips], PLANE, pair_recv.at[2, i])
        for j in range(COLS // 128):
            four = [r_all[j % CORES, plane(i) * PLANE + j // CORES * PAIR + r] for r in range(PAIR)]
            block = jnp.concatenate([regroup(four, r) for r in range(GROUPS)], axis=0)
            put_parts(b_parts, slice(i * COLS + j * 128, i * COLS + j * 128 + 128), block)

    def some_columns(i, rows):
        columns = pl.ds(pl.multiple_of(plane(i) * COLS, COLS), COLS)
        parts = b_parts[0:PARTS * RANK, i * COLS:i * COLS + COLS]
        acc = lax.dot_general(parts, g[rows, columns], NT, preferred_element_type=F32)
        acc = acc + lax.dot_general(parts, e[rows, columns], NT, preferred_element_type=F32)
        return add_parts(acc)

    def columns_step(i, r):
        rows = slice(r, r + ROWS2)
        if i == 0:
            left[:, rows] = some_columns(i, rows)
        else:
            left[:, rows] += some_columns(i, rows)

    for i in range(STEPS_X):
        if i == 2:
            wait_tiles(r_all.at[0], 2 * PLANE - 1, send_sem.at[6])
        send_right(i)
    pass_on(0)
    unpack(0)
    for i in range(STEPS_X - 1):
        pass_on(i + 1)
        columns_step(i, 0)
        unpack(i + 1)
        for r in range(ROWS2, D, ROWS2):
            columns_step(i, r)

    def last_columns(i, carry):
        steps = D // ROWS2
        chunk = ((me * steps) // N + steps // 2 + i) % steps
        rows = pl.ds(pl.multiple_of(chunk * ROWS2, ROWS2), ROWS2)
        put_left(1, chunk, ROWS2, left[:, rows] + some_columns(STEPS_X - 1, rows))
        send_left(1, chunk, ROWS2)
        return carry

    lax.fori_loop(0, D // ROWS2, last_columns, 0)
    inverse = inverse_factor(b_parts)
    send_left_sums(1)
    for j in range(D // 512):
        block = jnp.concatenate(
            [
                jnp.concatenate([l_all[1, (j * 4 + i) * GROUPS + r] for r in range(GROUPS)], axis=0)
                for i in range(4)
            ],
            axis=1,
        )
        block = jnp.dot(inverse, block, precision=EXACT, preferred_element_type=F32)
        left[:, j * 512:j * 512 + 512] = block
        put_parts(l_parts, slice(j * 512, j * 512 + 512), block)
    right_product(1)
    at = (me * OUT_L) // 128
    block = left[:, pl.ds(pl.multiple_of(at * 128, 128), 256)]
    block = pltpu.roll(block, (256 - (me * OUT_L - at * 128)) % 256, 1)[:, 0:128]
    out[0:OUT_L, :] = block.T[0:OUT_L, :]
    inverse = inverse_factor(l_parts)
    mine = right_sum(1, inverse)
    out[OUT_AT:OUT_AT + OUT_R, :] = mine.T[0:OUT_R, :]

    for it in range(2):
        @pl.when(owns_left)
        def _():
            wait_tiles(l_send.at[it], TL - 1, send_sem.at[2 * it])
            wait_tiles(l_recv.at[it], N - 1, send_sem.at[4 + it])

        @pl.when(jnp.logical_not(owns_left))
        def _():
            wait_tiles(l_send.at[it], TL, send_sem.at[2 * it])

        wait_tiles(r_half.at[it], CHIPS - 1, send_sem.at[2 * it + 1])
        wait_tiles(r_pair.at[it], CHIPS, pair_send.at[it])
    wait_tiles(r_all.at[0], 2 * PLANE, far_send)
    wait_tiles(r_all.at[0], CHIPS, pair_send.at[2])


def hand_out(both, left, right):
    left[...] = both[0:OUT_L, :]
    right[...] = both[OUT_AT:OUT_AT + OUT_R, :]


def shards(local_grads, error_feedback, q_start):
    anywhere = pl.BlockSpec(memory_space=pl.ANY)
    vmem = pl.BlockSpec(memory_space=pltpu.VMEM)
    out = pl.pallas_call(
        kernel,
        out_shape=jax.ShapeDtypeStruct((OUT_AT + OUT_R, RANK), F32),
        in_specs=[anywhere, anywhere, anywhere],
        out_specs=vmem,
        scratch_shapes=[
            pltpu.VMEM((D, FF), BF16),
            pltpu.VMEM((D, FF), BF16),
            pltpu.VMEM((RANK, FF), F32),
            pltpu.VMEM((128, FF), BF16),
            pltpu.VMEM((128, D), BF16),
            pltpu.VMEM((2, TL, 8, 128), F32),
            pltpu.VMEM((2, N, 8, 128), F32),
            pltpu.VMEM((2, TL, 8, 128), F32),
            pltpu.VMEM((2, CORES, CHIPS, 8, 128), F32),
            pltpu.VMEM((2, CHIPS, 8, 128), F32),
            pltpu.VMEM((2, CHIPS, 8, 128), F32),
            pltpu.VMEM((2, CHIPS, 8, 128), F32),
            pltpu.VMEM((CORES, CHIPS, 8, 128), F32),
            pltpu.VMEM((3, 8, 128), F32),
            pltpu.VMEM((RANK, D + 128), F32),
            pltpu.SemaphoreType.DMA((2 * (D // ROWS) + 1,)),
            pltpu.SemaphoreType.DMA((7,)),
            pltpu.SemaphoreType.DMA(()),
            pltpu.SemaphoreType.DMA((6 + X,)),
            pltpu.SemaphoreType.DMA((3,)),
            pltpu.SemaphoreType.DMA((3, STEPS_X)),
        ],
        compiler_params=pltpu.CompilerParams(
            vmem_limit_bytes=60 << 20, collective_id=0, has_side_effects=True
        ),
    )(local_grads, error_feedback, q_start.T)
    return pl.pallas_call(
        hand_out,
        out_shape=(
            jax.ShapeDtypeStruct((OUT_L, RANK), F32),
            jax.ShapeDtypeStruct((OUT_R, RANK), F32),
        ),
    )(out)


def solution(mesh):
    return jax.shard_map(
        shards,
        mesh=mesh,
        in_specs=(P(("dp", "pair"), None, None), P(("dp", "pair"), None, None), P()),
        out_specs=(P(("dp", "pair"), None), P(("dp", "pair"), None)),
        check_vma=False,
    )
```
